32 devices in a mesh: rep: 8 (over z, y), fsdp: 2 (over x), ctx: 2 (over core).
Axes of the slice: x: 2, y: 2, z: 4, core: 2. Of those that a mesh axis runs over, the one named last changes fastest.
Arguments:
- tokens: bfloat16 [32, 1024, 1280], P(('rep', 'fsdp'), 'ctx'), may hold values from -6 to 6
- prefixes: int32 [32], P(('rep', 'fsdp')), may hold values from 102 to 512, as said below
- query_weight: bfloat16 [1280, 1280], P(('fsdp', 'ctx')), may hold values from -0.15625 to 0.15625
- key_weight: bfloat16 [1280, 1280], P(('fsdp', 'ctx')), may hold values from -0.15625 to 0.15625
- value_weight: bfloat16 [1280, 1280], P(('fsdp', 'ctx')), may hold values from -0.15625 to 0.15625
- output_weight: bfloat16 [1280, 1280], P(('fsdp', 'ctx')), may hold values from -2 to 2
- up_weight: bfloat16 [1280, 1280], P(('fsdp', 'ctx')), may hold values from -0.15625 to 0.15625
- up_bias: float32 [1280], replicated, may hold values from -3 to 3
- down_weight: bfloat16 [1280, 1280], P(('fsdp', 'ctx')), may hold values from -0.15625 to 0.15625
- down_bias: float32 [1280], replicated, may hold values from -3 to 3
- attn_gain: float32 [1280], replicated, may hold values from 0.5 to 1.5
- mlp_gain: float32 [1280], replicated, may hold values from 0.5 to 1.5
- query_scale: float32 [80], replicated, may hold values from -2.5 to 2.5
- cotangent: bfloat16 [32, 1024, 1280], P(('rep', 'fsdp'), 'ctx'), may hold values from -6 to 6
Outputs:
- mixed: bfloat16 [32, 1024, 1280], P(('rep', 'fsdp'), 'ctx')
- tokens_grad: bfloat16 [32, 1024, 1280], P(('rep', 'fsdp'), 'ctx')
- query_grad: float32 [1280, 1280], P(('fsdp', 'ctx'))
- key_grad: float32 [1280, 1280], P(('fsdp', 'ctx'))
- value_grad: float32 [1280, 1280], P(('fsdp', 'ctx'))
- output_grad: float32 [1280, 1280], P(('fsdp', 'ctx'))
- up_grad: float32 [1280, 1280], P(('fsdp', 'ctx'))
- upbias_grad: float32 [1280], replicated
- down_grad: float32 [1280, 1280], P(('fsdp', 'ctx'))
- downbias_grad: float32 [1280], replicated
- attngain_grad: float32 [1280], replicated
- mlpgain_grad: float32 [1280], replicated
- scale_grad: float32 [80], replicated
The draws below stay inside these ranges and needn't reach their ends.
Inputs may be any that keep to these rules, and one draw needn't show every extreme that they name: `prefixes`: at least one sequence has 1024 // 10 and one has 1024 // 2.
All inputs are finite; a program needn't handle non-finite values.
Results may differ from the reference program's by a relative error of at most 0.02.
Values may be sent and summed in bfloat16 or wider, within the bound.
No kernel may reach another device: no remote copies, remote signals or barrier semaphores. Data moves between devices by JAX's collectives and lax.ppermute only.
A program may use at most 384 MiB of HBM per device.

```python
import jax
import jax.numpy as jnp
from jax import lax

D = 1280
HD = 80
FF = 1280
SEQ_LEN = 1024
SEQUENCES = 32


def draw_prefixes(key, part):
    least_prefix = SEQ_LEN // 10
    most_prefix = SEQ_LEN // 2
    key_values, key_top, key_least = jax.random.split(key, 3)
    lengths = jax.random.randint(key_values, (SEQUENCES,), least_prefix, most_prefix + 1, dtype=jnp.int32)
    top_spot = jax.random.randint(key_top, (), 0, SEQUENCES, dtype=jnp.int32)
    least_spot = (top_spot + 1 + jax.random.randint(key_least, (), 0, SEQUENCES - 1, dtype=jnp.int32)) % SEQUENCES
    positions = jnp.arange(SEQUENCES, dtype=jnp.int32)
    lengths = jnp.where(positions == top_spot, most_prefix, lengths)
    return jnp.where(positions == least_spot, least_prefix, lengths)


def block_scale(key, shape, pieces, low, largest):
    def one(axis_at, shards_of):
        steps = jax.random.uniform(jax.random.fold_in(jax.random.fold_in(key, 6), axis_at), (shards_of,), jnp.float32, low / len(pieces), largest / len(pieces))
        return jnp.repeat(jnp.exp(steps), shape[axis_at] // shards_of).reshape((-1,) + (1,) * (len(shape) - axis_at - 1))

    level = one(*pieces[0])
    for cut in pieces[1:]:
        level = level * one(*cut)
    return level


def noise(rng, extent, width, bound, cuts=(), held_as=jnp.bfloat16):
    values = jax.random.normal(rng, extent, jnp.float32) * width
    if len(cuts) > 0:
        values = block_scale(rng, extent, cuts, -0.22, 0.18) * values
    return jnp.clip(values, min=-bound, max=bound).astype(held_as)


def setup_inputs(seed: int = 0) -> dict:
    splits = jax.random.split(jax.random.key(seed), 15)
    return {
        "tokens": noise(splits[0], (SEQUENCES, SEQ_LEN, D), 1.0, 6.0, ((0, 16), (1, 2))),
        "prefixes": draw_prefixes(jax.random.fold_in(splits[14], 71), 0),
        "query_weight": noise(splits[2], (D, D), D ** -0.5, 0.15625, ((0, 4),)),
        "key_weight": noise(splits[3], (D, D), D ** -0.5, 0.15625, ((0, 4),)),
        "value_weight": noise(splits[4], (D, D), D ** -0.5, 0.15625, ((0, 4),)),
        "output_weight": noise(splits[5], (D, D), (max(D // 128, 1)) ** -0.5, 2.0, ((0, 4),)),
        "up_weight": noise(splits[6], (D, FF), D ** -0.5, 0.15625, ((0, 4),)),
        "up_bias": noise(splits[7], (FF,), 0.5, 3.0, (), jnp.float32),
        "down_weight": noise(splits[8], (FF, D), FF ** -0.5, 0.15625, ((0, 4),)),
        "down_bias": noise(splits[9], (D,), 0.5, 3.0, (), jnp.float32),
        "attn_gain": jnp.clip(1.0 + 0.1 * jax.random.normal(splits[10], (D,), jnp.float32), 0.5, 1.5),
        "mlp_gain": jnp.clip(1.0 + 0.1 * jax.random.normal(splits[11], (D,), jnp.float32), 0.5, 1.5),
        "query_scale": noise(splits[12], (HD,), 0.5, 2.5, (), jnp.float32),
        "cotangent": noise(splits[13], (SEQUENCES, SEQ_LEN, D), 1.0, 6.0, ((0, 16), (1, 2))),
    }


epsilon = 1e-06
softplus_gain = 1.442695041
highest = lax.Precision.HIGHEST

@jax.custom_vjp
def low(v):
    return lax.optimization_barrier(v.astype(jnp.bfloat16)).astype(jnp.float32)

@jax.custom_vjp
def low_back(v):
    return v

def low_keep(v):
    return (low(v), None)

def low_pass(kept, grad):
    return (grad,)

def back_keep(v):
    return (v, None)

def back_low(kept, grad):
    return (low(grad),)
low.defvjp(low_keep, low_pass)
low_back.defvjp(back_keep, back_low)

def product(left, right):
    return jnp.dot(left, right, precision=highest)

def rms_norm(values, gain_vec):
    factor = lax.rsqrt(lax.optimization_barrier(jnp.mean(values * values, axis=-1, keepdims=True)) + epsilon)
    return values * factor * gain_vec

def attend(queries, keys, values, prefix):
    scores = low_back(jnp.einsum('qhe,khe->hqk', queries, keys, precision=highest))
    length = queries.shape[0]
    row_index = jnp.arange(length, dtype=jnp.int32)[:, None]
    col_index = jnp.arange(length, dtype=jnp.int32)[None, :]
    allowed = (col_index <= row_index) | (col_index < prefix)
    scores = jnp.where(allowed[None], scores, -1e+30)
    row_max = lax.optimization_barrier(jnp.max(scores, axis=-1, keepdims=True))
    weights = jnp.exp(scores - row_max)
    probability = low(weights / lax.optimization_barrier(jnp.sum(weights, axis=-1, keepdims=True)))
    return jnp.einsum('hqk,khe->qhe', probability, values, precision=highest)

def forward(tokens, query_weight, key_weight, value_weight, output_weight, up_weight, up_bias, down_weight, down_bias, attn_gain, mlp_gain, query_scale, prefixes):
    seq_count, length, model_width = tokens.shape
    head_count = model_width // HD
    rows_in = tokens.reshape(seq_count * length, model_width)
    normed = low(rms_norm(rows_in, attn_gain))
    factor = jax.nn.softplus(query_scale) * (softplus_gain * HD ** (-0.5))
    queries = low_back(product(normed, query_weight)).reshape(seq_count, length, head_count, HD)
    queries = low_back(low(queries * factor))
    keys = low_back(low(product(normed, key_weight))).reshape(seq_count, length, head_count, HD)
    values = low_back(low(product(normed, value_weight))).reshape(seq_count, length, head_count, HD)
    context = lax.map(lambda members: jax.checkpoint(attend)(*members), (queries, keys, values, prefixes))
    attended = low_back(low(context.reshape(seq_count * length, model_width)))
    middle = rows_in + low_back(product(attended, output_weight))
    normed_two = low(rms_norm(middle, mlp_gain))
    before = low_back(product(normed_two, up_weight) + up_bias)
    hidden = low(jax.nn.silu(before))
    result = middle + product(hidden, down_weight) + down_bias
    return result.reshape(seq_count, length, model_width)

def reference(tokens, prefixes, query_weight, key_weight, value_weight, output_weight, up_weight, up_bias, down_weight, down_bias, attn_gain, mlp_gain, query_scale, cotangent):
    operands = [array.astype(jnp.float32) for array in (tokens, query_weight, key_weight, value_weight, output_weight, up_weight, up_bias, down_weight, down_bias, attn_gain, mlp_gain, query_scale)]

    def wrapped(*inputs):
        return forward(*inputs, prefixes)
    result, pullback = jax.vjp(wrapped, *operands)
    grads = pullback(cotangent.astype(jnp.float32))
    return (result.astype(jnp.bfloat16), grads[0].astype(jnp.bfloat16), grads[1], grads[2], grads[3], grads[4], grads[5], grads[6], grads[7], grads[8], grads[9], grads[10], grads[11])
```

```python
import functools

import jax
import jax.numpy as jnp
from jax import lax
from jax.experimental import pallas as pl
from jax.experimental.pallas import tpu as pltpu
from jax.sharding import PartitionSpec as P

HD = 80
LANES = 128
WIN = 256
QB = 256

epsilon = 1e-06
softplus_gain = 1.442695041
masked_value = -1e30


def norm_factor(values):
    return lax.rsqrt(jnp.mean(values * values, axis=-1, keepdims=True) + epsilon)


def norm_back(upstream, values, factor, gain_vec):
    scaled = upstream * gain_vec
    row_inner = jnp.mean(scaled * values, axis=-1, keepdims=True)
    return factor * scaled - values * factor**3 * row_inner


def dot_nt(a, b):
    return lax.dot_general(a, b, (((1,), (1,)), ((), ())), preferred_element_type=jnp.float32)


def dot_nn(a, b):
    return lax.dot_general(a, b, (((1,), (0,)), ((), ())), preferred_element_type=jnp.float32)


def head_window(head, cols):
    start = jnp.minimum((head * HD) // LANES, cols // LANES - WIN // LANES)
    off = head * HD - start * LANES
    lane = lax.broadcasted_iota(jnp.int32, (1, WIN), 1)
    mask = (lane >= off) & (lane < off + HD)
    return pl.ds(pl.multiple_of(start * LANES, LANES), WIN), mask


def key_extent(block, half):
    return max(half, (block + 1) * QB)


def score_blocks(kw, qm, block, prefix, half):
    extent = key_extent(block, half)
    scores = dot_nt(kw[:extent], qm[block * QB : (block + 1) * QB])
    row = lax.broadcasted_iota(jnp.int32, (QB, QB), 0)
    col = lax.broadcasted_iota(jnp.int32, (QB, QB), 1)
    pieces = []
    for kb in range(extent // QB):
        piece = scores[kb * QB : (kb + 1) * QB]
        in_prefix = (row + kb * QB) < prefix
        if kb == block:
            allowed = row <= col
            if (kb * QB) < half:
                allowed = allowed | in_prefix
            piece = jnp.where(allowed, piece, masked_value)
        elif kb > block:
            piece = jnp.where(in_prefix, piece, masked_value)
        pieces.append(piece)
    return pieces


def forward_kernel(
    prefix_ref, place_ref,
    q_own, k_own, v_own, q_oth, k_oth, v_oth,
    o_own, o_oth, lse_ref,
    qs, ks, vs, os,
):
    seq, head = pl.program_id(0), pl.program_id(1)
    heads = pl.num_programs(1)
    half, cols = q_own.shape[1:]
    mine = pl.ds(pl.multiple_of(place_ref[0] * half, half), half)
    others = pl.ds(pl.multiple_of((1 - place_ref[0]) * half, half), half)

    @pl.when(head == 0)
    def _():
        for dst, a, b in ((qs, q_own, q_oth), (ks, k_own, k_oth), (vs, v_own, v_oth)):
            dst[mine, :] = a[0]
            dst[others, :] = b[0]

    prefix = prefix_ref[seq]
    win, mask = head_window(head, cols)
    kw = ks[:, win]
    zero = jnp.zeros((), qs.dtype)
    qm = jnp.where(mask, qs[:, win], zero)
    vt = vs[:, win].T
    for block in range(2 * half // QB):
        rows = slice(block * QB, (block + 1) * QB)
        pieces = score_blocks(kw, qm, block, prefix, half)
        top = functools.reduce(jnp.maximum, [jnp.max(p, axis=0, keepdims=True) for p in pieces])
        weights = [jnp.exp(p - top) for p in pieces]
        total = sum(jnp.sum(p, axis=0, keepdims=True) for p in weights)
        packed = jnp.concatenate([p.astype(jnp.bfloat16) for p in weights], axis=0)
        out_t = dot_nn(vt[:, : packed.shape[0]], packed) * (1.0 / total)
        out = out_t.T
        os[rows, win] = jnp.where(mask, out.astype(jnp.bfloat16), os[rows, win])
        lse_ref[0, pl.ds(head, 1), rows] = top + jnp.log(total)

    @pl.when(head == heads - 1)
    def _():
        o_own[0] = os[mine, :]
        o_oth[0] = os[others, :]


def backward_kernel(
    prefix_ref, place_ref,
    q_own, k_own, v_own, g_own, o_own, q_oth, k_oth, v_oth, g_oth, o_oth, lse_ref, ind_ref,
    dq_own, dk_own, dv_own, dq_oth, dk_oth, dv_oth,
    qs, ks, vs, gs, dqs, dks, dvs, pbuf, sbuf, delta,
):
    seq, head = pl.program_id(0), pl.program_id(1)
    heads = pl.num_programs(1)
    half, cols = q_own.shape[1:]
    mine = pl.ds(pl.multiple_of(place_ref[0] * half, half), half)
    others = pl.ds(pl.multiple_of((1 - place_ref[0]) * half, half), half)

    @pl.when(head == 0)
    def _():
        for dst, a, b in ((qs, q_own, q_oth), (ks, k_own, k_oth), (vs, v_own, v_oth), (gs, g_own, g_oth)):
            dst[mine, :] = a[0]
            dst[others, :] = b[0]
        for where_, g, o in ((mine, g_own, o_own), (others, g_oth, o_oth)):
            product = g[0].astype(jnp.float32) * o[0].astype(jnp.float32)
            high = product.astype(jnp.bfloat16)
            low = (product - high.astype(jnp.float32)).astype(jnp.bfloat16)
            delta[:, where_] = dot_nt(ind_ref[...], high) + dot_nt(ind_ref[...], low)

    prefix = prefix_ref[seq]
    win, mask = head_window(head, cols)
    zero = jnp.zeros((), qs.dtype)
    kw = ks[:, win]
    vw = vs[:, win]
    qm = jnp.where(mask, qs[:, win], zero)
    gm = jnp.where(mask, gs[:, win], zero)
    kt = kw.T
    blocks = 2 * half // QB
    for block in range(blocks):
        rows = slice(block * QB, (block + 1) * QB)
        extent = key_extent(block, half)
        pieces = score_blocks(kw, qm, block, prefix, half)
        pgrad = dot_nt(vw[:extent], gm[rows])
        lse = lse_ref[0, pl.ds(head, 1), rows]
        inner = delta[pl.ds(head, 1), rows]
        for kb, piece in enumerate(pieces):
            prob = jnp.exp(piece - lse)
            keys = slice(kb * QB, (kb + 1) * QB)
            pbuf[keys, rows] = prob.astype(jnp.bfloat16)
            sbuf[keys, rows] = (prob * (pgrad[keys] - inner)).astype(jnp.bfloat16)
        dq = dot_nn(kt[:, :extent], sbuf[:extent, rows]).T
        dqs[rows, win] = jnp.where(mask, dq.astype(jnp.bfloat16), dqs[rows, win])
    for kb in range(blocks):
        keys = slice(kb * QB, (kb + 1) * QB)
        first = 0 if kb * QB < half else kb * QB
        dv = dot_nn(pbuf[keys, first:], gm[first:])
        dvs[keys, win] = jnp.where(mask, dv.astype(jnp.bfloat16), dvs[keys, win])
        dk = dot_nn(sbuf[keys, first:], qm[first:])
        dks[keys, win] = jnp.where(mask, dk.astype(jnp.bfloat16), dks[keys, win])

    @pl.when(head == heads - 1)
    def _():
        for src, a, b in ((dqs, dq_own, dq_oth), (dks, dk_own, dk_oth), (dvs, dv_own, dv_oth)):
            a[0] = src[mine, :]
            b[0] = src[others, :]


def seq_spec(half, cols):
    return pl.BlockSpec((1, half, cols), lambda s, h, *_: (s, 0, 0))


def attention_forward(prefixes, place, own, oth):
    seqs, half, cols = own[0].shape
    heads = cols // HD
    spec = seq_spec(half, cols)
    piece = jax.ShapeDtypeStruct((seqs, half, cols), jnp.bfloat16)
    length = 2 * half
    cells = seqs * heads * length * length
    return pl.pallas_call(
        forward_kernel,
        out_shape=(piece, piece, jax.ShapeDtypeStruct((seqs, heads, length), jnp.float32)),
        grid_spec=pltpu.PrefetchScalarGridSpec(
            num_scalar_prefetch=2,
            grid=(seqs, heads),
            in_specs=[spec] * 6,
            out_specs=[spec, spec, pl.BlockSpec((1, heads, length), lambda s, h, *_: (s, 0, 0))],
            scratch_shapes=[pltpu.VMEM((length, cols), jnp.bfloat16)] * 4,
        ),
        compiler_params=pltpu.CompilerParams(
            dimension_semantics=("arbitrary", "arbitrary"), vmem_limit_bytes=56 << 20
        ),
        cost_estimate=pl.CostEstimate(
            flops=2 * cells * WIN * 2, transcendentals=cells, bytes_accessed=8 * seqs * half * cols * 2
        ),
        name="attention_forward",
    )(prefixes, place, *own, *oth)


def attention_backward(prefixes, place, own, oth, lse):
    seqs, half, cols = own[0].shape
    heads = cols // HD
    spec = seq_spec(half, cols)
    piece = jax.ShapeDtypeStruct((seqs, half, cols), jnp.bfloat16)
    length = 2 * half
    cells = seqs * heads * length * length
    indicator = (
        jnp.arange(heads, dtype=jnp.int32)[:, None] == (jnp.arange(cols, dtype=jnp.int32) // HD)[None, :]
    ).astype(jnp.bfloat16)
    return pl.pallas_call(
        backward_kernel,
        out_shape=(piece,) * 6,
        grid_spec=pltpu.PrefetchScalarGridSpec(
            num_scalar_prefetch=2,
            grid=(seqs, heads),
            in_specs=[spec] * 10
            + [
                pl.BlockSpec((1, heads, length), lambda s, h, *_: (s, 0, 0)),
                pl.BlockSpec((heads, cols), lambda s, h, *_: (0, 0)),
            ],
            out_specs=[spec] * 6,
            scratch_shapes=[pltpu.VMEM((length, cols), jnp.bfloat16)] * 7
            + [pltpu.VMEM((length, length), jnp.bfloat16)] * 2
            + [pltpu.VMEM((heads, length), jnp.float32)],
        ),
        compiler_params=pltpu.CompilerParams(
            dimension_semantics=("arbitrary", "arbitrary"), vmem_limit_bytes=60 << 20
        ),
        cost_estimate=pl.CostEstimate(
            flops=2 * cells * WIN * 5, transcendentals=cells, bytes_accessed=16 * seqs * half * cols * 2
        ),
        name="attention_backward",
    )(prefixes, place, *own, *oth, lse, indicator)


def swap(value, axis, size, bit=1):
    return lax.ppermute(value, axis, [(i, i ^ bit) for i in range(size)])


def pick(value, index, axis=0):
    return lax.dynamic_index_in_dim(value, index, axis, keepdims=False)


def in_order(bit, mine, theirs, axis=0):
    low = jnp.where(bit == 0, mine, theirs)
    high = jnp.where(bit == 0, theirs, mine)
    return jnp.stack([low, high], axis=axis)


class Place:
    def __init__(self, sizes):
        self.reps, self.groups, self.cores = sizes
        self.rep = lax.axis_index("rep")
        self.group = lax.axis_index("fsdp")
        self.core = lax.axis_index("ctx")
        self.paired = self.groups == 2 and self.cores == 2 and self.reps == 8


def gather_rows(place, shard):
    if not place.paired:
        return lax.all_gather(shard, ("fsdp", "ctx"), axis=0, tiled=True)
    rows, cols = shard.shape
    near = place.rep & 1
    halves = shard.reshape(2, rows // 2, cols)
    got = swap(pick(halves, near), "fsdp", 2)
    more = swap(got, "rep", place.reps, 1)
    partner = in_order(near, got, more).reshape(rows, cols)
    both = in_order(place.group, shard, partner)
    beside = swap(both, "ctx", 2)
    return in_order(place.core, both, beside, axis=1).reshape(4 * rows, cols)


def chip_sum(place, partial, flipped=False):
    total_rows, cols = partial.shape
    rows = total_rows // (place.groups * 2)
    blocks = partial.reshape(place.groups, 2, rows, cols)
    got = swap(pick(blocks, 1 - place.core, 1), "ctx", 2)
    if flipped:
        got = jnp.roll(got, cols // 2, axis=-1)
    return (pick(blocks, place.core, 1).astype(jnp.float32) + got.astype(jnp.float32)).astype(jnp.bfloat16)


def spread_sum(place, value, order):
    groups, rows, cols = value.shape
    if not place.paired:
        mine = lax.psum_scatter(value, "fsdp", scatter_dimension=0, tiled=True)[0]
        return lax.psum(mine, "rep").astype(jnp.float32)
    bits = {"x": place.group, "y": place.rep & 1, "z": (place.rep >> 1) & 1}
    send = {
        "x": lambda v: swap(v, "fsdp", 2),
        "y": lambda v: swap(v, "rep", place.reps, 1),
        "z": lambda v: swap(v, "rep", place.reps, 2),
    }
    held = value.reshape(2, 2, 2, rows // 4, cols)
    axes = ["x", "y", "z"]
    for name in order:
        at = axes.index(name)
        got = send[name](pick(held, 1 - bits[name], at))
        held = (pick(held, bits[name], at).astype(jnp.float32) + got.astype(jnp.float32)).astype(jnp.bfloat16)
        axes.pop(at)
    held = (held.astype(jnp.float32) + swap(held, "rep", place.reps, 4).astype(jnp.float32)).astype(jnp.bfloat16)
    gathered = [name for name in reversed(order) if name != "x"]
    present = []
    for name in gathered:
        at = sum(1 for other in present if other < name)
        held = in_order(bits[name], held, send[name](held), axis=at)
        present.append(name)
    return held.reshape(rows, cols).astype(jnp.float32)


def everywhere_sum(place, value):
    if not place.paired:
        return lax.psum(value, ("rep", "fsdp", "ctx"))
    value = value + swap(value, "ctx", 2)
    value = value + swap(value, "fsdp", 2)
    for bit in (1, 2, 4):
        value = value + swap(value, "rep", place.reps, bit)
    return value


def shards(
    sizes,
    tokens,
    prefixes,
    query_weight,
    key_weight,
    value_weight,
    output_weight,
    up_weight,
    up_bias,
    down_weight,
    down_bias,
    attn_gain,
    mlp_gain,
    query_scale,
    cotangent,
):
    place = Place(sizes)
    core = place.core
    seq_count, local_rows, width = tokens.shape
    count = seq_count * local_rows
    part = width // 2
    heads_part = part // HD
    core_arg = core.astype(jnp.int32).reshape(1)

    key_full = gather_rows(place, key_weight)
    value_full = gather_rows(place, value_weight)
    query_full = gather_rows(place, query_weight)
    output_full = gather_rows(place, output_weight)
    up_full = gather_rows(place, up_weight)
    down_full = gather_rows(place, down_weight)

    def columns(matrix, which):
        return lax.dynamic_slice_in_dim(matrix, which * part, part, axis=1)

    rows_in = tokens.reshape(count, width).astype(jnp.float32)
    factor_one = norm_factor(rows_in)
    normed = (rows_in * factor_one * attn_gain).astype(jnp.bfloat16)
    scale_soft = jax.nn.softplus(query_scale) * (softplus_gain * HD ** (-0.5))
    scale_part_row = jnp.tile(scale_soft, heads_part)

    key_w = [columns(key_full, core), columns(key_full, 1 - core)]
    value_w = [columns(value_full, core), columns(value_full, 1 - core)]
    query_w = [columns(query_full, core), columns(query_full, 1 - core)]

    def split(value):
        return value.reshape(seq_count, local_rows, part)

    key_own, key_snd = [dot_nn(normed, w).astype(jnp.bfloat16) for w in key_w]
    key_oth = swap(key_snd, "ctx", 2)
    value_own, value_snd = [dot_nn(normed, w).astype(jnp.bfloat16) for w in value_w]
    value_oth = swap(value_snd, "ctx", 2)
    raw_own, raw_snd = [dot_nn(normed, w) for w in query_w]
    query_own, query_snd = [(raw * scale_part_row).astype(jnp.bfloat16) for raw in (raw_own, raw_snd)]
    query_oth = swap(query_snd, "ctx", 2)

    own = [split(v) for v in (query_own, key_own, value_own)]
    oth = [split(v) for v in (query_oth, key_oth, value_oth)]
    out_own, out_snd, lse = attention_forward(prefixes, core_arg, own, oth)
    out_rcv = swap(out_snd, "ctx", 2)

    attended = [out_own.reshape(count, part), out_rcv.reshape(count, part)]
    output_w = [
        lax.dynamic_slice_in_dim(output_full, core * part, part, axis=0),
        lax.dynamic_slice_in_dim(output_full, (1 - core) * part, part, axis=0),
    ]
    middle = rows_in + dot_nn(attended[0], output_w[0]) + dot_nn(attended[1], output_w[1])
    factor_two = norm_factor(middle)
    normed_two = (middle * factor_two * mlp_gain).astype(jnp.bfloat16)
    before = dot_nn(normed_two, up_full) + up_bias
    gate_sig = jax.nn.sigmoid(before)
    hidden = (before * gate_sig).astype(jnp.bfloat16)
    mixed_rows = middle + dot_nn(hidden, down_full) + down_bias
    mixed_out = mixed_rows.astype(jnp.bfloat16).reshape(seq_count, local_rows, width)

    upstream = cotangent.reshape(count, width)
    upstream_wide = upstream.astype(jnp.float32)

    def weight_grad(left, right):
        return lax.dot_general(
            left, right, (((0,), (0,)), ((), ())), preferred_element_type=jnp.float32
        ).astype(jnp.bfloat16)

    down_part = weight_grad(hidden, upstream)
    down_total = spread_sum(place, chip_sum(place, down_part), "xyz")
    downbias_part = jnp.sum(upstream_wide, axis=0)
    hidden_grad = dot_nt(upstream, down_full)
    before_grad = (hidden_grad * gate_sig * (1.0 + before * (1.0 - gate_sig))).astype(jnp.bfloat16)
    up_part = weight_grad(normed_two, before_grad)
    up_total = spread_sum(place, chip_sum(place, up_part), "yzx")
    upbias_part = jnp.sum(before_grad.astype(jnp.float32), axis=0)
    normed_grad = dot_nt(before_grad, up_full)
    mlpgain_part = jnp.sum(normed_grad * middle * factor_two, axis=0)
    middle_grad = upstream_wide + norm_back(normed_grad, middle, factor_two, mlp_gain)
    middle_low = middle_grad.astype(jnp.bfloat16)
    grad_own = dot_nt(middle_low, output_w[0]).astype(jnp.bfloat16)
    grad_snd = dot_nt(middle_low, output_w[1]).astype(jnp.bfloat16)
    grad_oth = swap(grad_snd, "ctx", 2)
    output_part = [weight_grad(a, middle_low) for a in attended]
    output_natural = in_order(core, output_part[0], output_part[1]).reshape(width, width)
    output_total = spread_sum(place, chip_sum(place, output_natural), "zxy")
    early = everywhere_sum(place, jnp.stack([upbias_part, downbias_part, mlpgain_part]))

    back = attention_backward(
        prefixes,
        core_arg,
        own + [split(grad_own), out_own],
        oth + [split(grad_oth), out_snd],
        lse,
    )
    dq_own, dk_own, dv_own = [v.reshape(count, part) for v in back[:3]]
    dq_rcv, dk_rcv, dv_rcv = [swap(v, "ctx", 2).reshape(count, part) for v in back[3:]]

    raws = (raw_own, raw_snd)
    dqs = (dq_own, dq_rcv)
    low_q = [(g.astype(jnp.float32) * scale_part_row).astype(jnp.bfloat16) for g in dqs]
    scale_part = sum(
        jnp.sum((g.astype(jnp.float32) * raw).reshape(count, heads_part, HD), axis=(0, 1))
        for g, raw in zip(dqs, raws)
    )
    scale_part = scale_part * jax.nn.sigmoid(query_scale) * (softplus_gain * HD ** (-0.5))

    totals = []
    for pair, order in ((low_q, "xyz"), ((dk_own, dk_rcv), "yzx"), ((dv_own, dv_rcv), "zxy")):
        partial = jnp.concatenate([weight_grad(normed, g) for g in pair], axis=1)
        rel = spread_sum(place, chip_sum(place, partial, flipped=True), order)
        totals.append(jnp.where(core == 0, rel, jnp.roll(rel, part, axis=1)))
    query_total, key_total, value_total = totals

    normed_grad_one = sum(
        dot_nt(g, w)
        for grads, weights in ((low_q, query_w), ((dk_own, dk_rcv), key_w), ((dv_own, dv_rcv), value_w))
        for g, w in zip(grads, weights)
    )
    attngain_part = jnp.sum(normed_grad_one * rows_in * factor_one, axis=0)
    tokens_grad = middle_grad + norm_back(normed_grad_one, rows_in, factor_one, attn_gain)
    tokens_grad = tokens_grad.astype(jnp.bfloat16).reshape(seq_count, local_rows, width)
    late = everywhere_sum(place, jnp.concatenate([attngain_part, scale_part]))

    return (
        mixed_out,
        tokens_grad,
        query_total,
        key_total,
        value_total,
        output_total,
        up_total,
        early[0],
        down_total,
        early[1],
        late[:width],
        early[2],
        late[width:],
    )


def solution(mesh):
    sizes = (mesh.shape["rep"], mesh.shape["fsdp"], mesh.shape["ctx"])
    rows = P(("rep", "fsdp"), "ctx", None)
    weight = P(("fsdp", "ctx"), None)
    return jax.shard_map(
        functools.partial(shards, sizes),
        mesh=mesh,
        in_specs=(
            rows, P(("rep", "fsdp")), weight, weight, weight, weight, weight,
            P(), weight, P(), P(), P(), P(), rows,
        ),
        out_specs=(
            rows, rows, weight, weight, weight, weight, weight,
            P(), weight, P(), P(), P(), P(),
        ),
        check_vma=False,
    )
```

```python
import functools

import jax
import jax.numpy as jnp
from jax import lax
from jax.experimental import pallas as pl
from jax.experimental.pallas import tpu as pltpu
from jax.sharding import PartitionSpec as P

HD = 80
LANES = 128
WIN = 256
QB = 256

epsilon = 1e-06
softplus_gain = 1.442695041
masked_value = -1e30


def norm_factor(values):
    return lax.rsqrt(jnp.mean(values * values, axis=-1, keepdims=True) + epsilon)


def norm_back(upstream, values, factor, gain_vec):
    scaled = upstream * gain_vec
    row_inner = jnp.mean(scaled * values, axis=-1, keepdims=True)
    return factor * scaled - values * factor**3 * row_inner


def dot_nt(a, b):
    return lax.dot_general(a, b, (((1,), (1,)), ((), ())), preferred_element_type=jnp.float32)


def dot_nn(a, b):
    return lax.dot_general(a, b, (((1,), (0,)), ((), ())), preferred_element_type=jnp.float32)


def head_window(head, cols):
    start = jnp.minimum((head * HD) // LANES, cols // LANES - WIN // LANES)
    off = head * HD - start * LANES
    lane = lax.broadcasted_iota(jnp.int32, (1, WIN), 1)
    mask = (lane >= off) & (lane < off + HD)
    return pl.ds(pl.multiple_of(start * LANES, LANES), WIN), mask


def key_extent(block, half):
    return max(half, (block + 1) * QB)


def score_blocks(kw, qm, block, prefix, half):
    extent = key_extent(block, half)
    scores = dot_nt(kw[:extent], qm[block * QB : (block + 1) * QB])
    row = lax.broadcasted_iota(jnp.int32, (QB, QB), 0)
    col = lax.broadcasted_iota(jnp.int32, (QB, QB), 1)
    pieces = []
    for kb in range(extent // QB):
        piece = scores[kb * QB : (kb + 1) * QB]
        in_prefix = (row + kb * QB) < prefix
        if kb == block:
            allowed = row <= col
            if (kb * QB) < half:
                allowed = allowed | in_prefix
            piece = jnp.where(allowed, piece, masked_value)
        elif kb > block:
            piece = jnp.where(in_prefix, piece, masked_value)
        pieces.append(piece)
    return pieces


def forward_kernel(
    prefix_ref, place_ref,
    q_own, k_own, v_own, q_oth, k_oth, v_oth,
    o_own, o_oth, lse_ref,
    qs, ks, vs, os,
):
    seq, head = pl.program_id(0), pl.program_id(1)
    heads = pl.num_programs(1)
    half, cols = q_own.shape[1:]
    mine = pl.ds(pl.multiple_of(place_ref[0] * half, half), half)
    others = pl.ds(pl.multiple_of((1 - place_ref[0]) * half, half), half)

    @pl.when(head == 0)
    def _():
        for dst, a, b in ((qs, q_own, q_oth), (ks, k_own, k_oth), (vs, v_own, v_oth)):
            dst[mine, :] = a[0]
            dst[others, :] = b[0]

    prefix = prefix_ref[seq]
    win, mask = head_window(head, cols)
    kw = ks[:, win]
    zero = jnp.zeros((), qs.dtype)
    qm = jnp.where(mask, qs[:, win], zero)
    vt = vs[:, win].T
    for block in range(2 * half // QB):
        rows = slice(block * QB, (block + 1) * QB)
        pieces = score_blocks(kw, qm, block, prefix, half)
        top = functools.reduce(jnp.maximum, [jnp.max(p, axis=0, keepdims=True) for p in pieces])
        weights = [jnp.exp(p - top) for p in pieces]
        total = sum(jnp.sum(p, axis=0, keepdims=True) for p in weights)
        packed = jnp.concatenate([p.astype(jnp.bfloat16) for p in weights], axis=0)
        out_t = dot_nn(vt[:, : packed.shape[0]], packed) * (1.0 / total)
        out = out_t.T
        os[rows, win] = jnp.where(mask, out.astype(jnp.bfloat16), os[rows, win])
        lse_ref[0, pl.ds(head, 1), rows] = top + jnp.log(total)

    @pl.when(head == heads - 1)
    def _():
        o_own[0] = os[mine, :]
        o_oth[0] = os[others, :]


def backward_kernel(
    first_head, tiles, carried, prefix_ref, place_ref, *refs
):
    refs = list(refs)
    take = lambda n: [refs.pop(0) for _ in range(n)]
    q_own, k_own, v_own, g_own, o_own, q_oth, k_oth, v_oth, g_oth, o_oth = take(10)
    lse_ref, ind_ref, scale_ref = take(3)
    carry_in = take(3) if carried else None
    grads = take(3)
    carry_out = None if carried else take(3)
    sums_ref = take(1)[0]
    qs, ks, vs, gs, dqs, dks, dvs, pbuf, sbuf, delta = refs
    seq, head = pl.program_id(0), pl.program_id(1) + first_head
    half, cols = q_own.shape[1:]
    start, stop = tiles[0] * LANES, tiles[1] * LANES
    mine = pl.ds(pl.multiple_of(place_ref[0] * half, half), half)
    others = pl.ds(pl.multiple_of((1 - place_ref[0]) * half, half), half)

    @pl.when(pl.program_id(1) == 0)
    def _():
        for dst, a, b in ((qs, q_own, q_oth), (ks, k_own, k_oth), (vs, v_own, v_oth), (gs, g_own, g_oth)):
            dst[mine, :] = a[0]
            dst[others, :] = b[0]
        for where_, g, o in ((mine, g_own, o_own), (others, g_oth, o_oth)):
            product = g[0].astype(jnp.float32) * o[0].astype(jnp.float32)
            high = product.astype(jnp.bfloat16)
            low = (product - high.astype(jnp.float32)).astype(jnp.bfloat16)
            delta[:, where_] = dot_nt(ind_ref[...], high) + dot_nt(ind_ref[...], low)
        if carried:
            for src, dst in zip(carry_in, (dqs, dks, dvs)):
                dst[mine, start : start + LANES] = src[0, 0]
                dst[others, start : start + LANES] = src[1, 0]

    @pl.when((seq == 0) & (pl.program_id(1) == 0))
    def _():
        sums_ref[...] = jnp.zeros_like(sums_ref)

    prefix = prefix_ref[seq]
    win, mask = head_window(head, cols)
    zero = jnp.zeros((), qs.dtype)
    kw = ks[:, win]
    vw = vs[:, win]
    qm = jnp.where(mask, qs[:, win], zero)
    gm = jnp.where(mask, gs[:, win], zero)
    kt = kw.T
    scale = scale_ref[:, win]
    blocks = 2 * half // QB
    for block in range(blocks):
        rows = slice(block * QB, (block + 1) * QB)
        extent = key_extent(block, half)
        pieces = score_blocks(kw, qm, block, prefix, half)
        pgrad = dot_nt(vw[:extent], gm[rows])
        lse = lse_ref[0, pl.ds(head, 1), rows]
        inner = delta[pl.ds(head, 1), rows]
        for kb, piece in enumerate(pieces):
            prob = jnp.exp(piece - lse)
            keys = slice(kb * QB, (kb + 1) * QB)
            pbuf[keys, rows] = prob.astype(jnp.bfloat16)
            sbuf[keys, rows] = (prob * (pgrad[keys] - inner)).astype(jnp.bfloat16)
        dq = dot_nn(kt[:, :extent], sbuf[:extent, rows]).T.astype(jnp.bfloat16).astype(jnp.float32)
        sums_ref[:, win] += jnp.sum(dq * qm[rows].astype(jnp.float32), axis=0, keepdims=True)
        dqs[rows, win] = jnp.where(mask, (dq * scale).astype(jnp.bfloat16), dqs[rows, win])
    for kb in range(blocks):
        keys = slice(kb * QB, (kb + 1) * QB)
        first = 0 if kb * QB < half else kb * QB
        dv = dot_nn(pbuf[keys, first:], gm[first:])
        dvs[keys, win] = jnp.where(mask, dv.astype(jnp.bfloat16), dvs[keys, win])
        dk = dot_nn(sbuf[keys, first:], qm[first:])
        dks[keys, win] = jnp.where(mask, dk.astype(jnp.bfloat16), dks[keys, win])

    @pl.when(pl.program_id(1) == pl.num_programs(1) - 1)
    def _():
        for i, src in enumerate((dqs, dks, dvs)):
            grads[i][0, 0] = src[mine, start:stop]
            grads[i][1, 0] = src[others, start:stop]
            if not carried:
                carry_out[i][0, 0] = src[mine, stop : stop + LANES]
                carry_out[i][1, 0] = src[others, stop : stop + LANES]


def seq_spec(half, cols):
    return pl.BlockSpec((1, half, cols), lambda s, h, *_: (s, 0, 0))


def attention_forward(prefixes, place, own, oth):
    seqs, half, cols = own[0].shape
    heads = cols // HD
    spec = seq_spec(half, cols)
    piece = jax.ShapeDtypeStruct((seqs, half, cols), jnp.bfloat16)
    length = 2 * half
    cells = seqs * heads * length * length
    return pl.pallas_call(
        forward_kernel,
        out_shape=(piece, piece, jax.ShapeDtypeStruct((seqs, heads, length), jnp.float32)),
        grid_spec=pltpu.PrefetchScalarGridSpec(
            num_scalar_prefetch=2,
            grid=(seqs, heads),
            in_specs=[spec] * 6,
            out_specs=[spec, spec, pl.BlockSpec((1, heads, length), lambda s, h, *_: (s, 0, 0))],
            scratch_shapes=[pltpu.VMEM((length, cols), jnp.bfloat16)] * 4,
        ),
        compiler_params=pltpu.CompilerParams(
            dimension_semantics=("arbitrary", "arbitrary"), vmem_limit_bytes=56 << 20
        ),
        cost_estimate=pl.CostEstimate(
            flops=2 * cells * WIN * 2, transcendentals=cells, bytes_accessed=8 * seqs * half * cols * 2
        ),
        name="attention_forward",
    )(prefixes, place, *own, *oth)


def attention_backward(prefixes, place, own, oth, lse, scale, heads_of, tiles, carry):
    seqs, half, cols = own[0].shape
    heads = cols // HD
    spec = seq_spec(half, cols)
    length = 2 * half
    cells = seqs * (heads_of[1] - heads_of[0]) * length * length
    indicator = (
        jnp.arange(heads, dtype=jnp.int32)[:, None] == (jnp.arange(cols, dtype=jnp.int32) // HD)[None, :]
    ).astype(jnp.bfloat16)

    def grad(width):
        shape = jax.ShapeDtypeStruct((2, seqs, half, width), jnp.bfloat16)
        return shape, pl.BlockSpec((2, 1, half, width), lambda s, h, *_: (0, s, 0, 0))

    width = (tiles[1] - tiles[0]) * LANES
    outs = [grad(width)] * 3 + ([] if carry else [grad(LANES)] * 3)
    outs.append((jax.ShapeDtypeStruct((1, cols), jnp.float32), pl.BlockSpec((1, cols), lambda s, h, *_: (0, 0))))
    return pl.pallas_call(
        functools.partial(backward_kernel, heads_of[0], tiles, bool(carry)),
        out_shape=[o[0] for o in outs],
        grid_spec=pltpu.PrefetchScalarGridSpec(
            num_scalar_prefetch=2,
            grid=(seqs, heads_of[1] - heads_of[0]),
            in_specs=[spec] * 10
            + [
                pl.BlockSpec((1, heads, length), lambda s, h, *_: (s, 0, 0)),
                pl.BlockSpec((heads, cols), lambda s, h, *_: (0, 0)),
                pl.BlockSpec((1, cols), lambda s, h, *_: (0, 0)),
            ]
            + [grad(LANES)[1]] * len(carry),
            out_specs=[o[1] for o in outs],
            scratch_shapes=[pltpu.VMEM((length, cols), jnp.bfloat16)] * 7
            + [pltpu.VMEM((length, length), jnp.bfloat16)] * 2
            + [pltpu.VMEM((heads, length), jnp.float32)],
        ),
        compiler_params=pltpu.CompilerParams(
            dimension_semantics=("arbitrary", "arbitrary"), vmem_limit_bytes=60 << 20
        ),
        cost_estimate=pl.CostEstimate(
            flops=2 * cells * WIN * 5, transcendentals=cells, bytes_accessed=16 * seqs * half * cols * 2
        ),
        name="attention_backward",
    )(prefixes, place, *own, *oth, lse, indicator, scale, *carry)


def input_grad_kernel(place_ref, *refs):
    *grads, wq, wk, wv, x_ref, mid_ref, gain_ref, out_ref, sums_ref = refs
    cols = wq.shape[1]
    part = cols // 2
    total = None
    pieces = iter(grads)
    for weight in (wq, wk, wv):
        for side in range(2):
            base = jnp.where(place_ref[0] == side, 0, part)
            at = 0
            for _ in range(2):
                piece = next(pieces)
                width = piece.shape[1]
                window = weight[:, pl.ds(pl.multiple_of(base + at, LANES), width)]
                term = dot_nt(piece[...], window)
                total = term if total is None else total + term
                at += width
    x = x_ref[...].astype(jnp.float32)
    factor = norm_factor(x)

    @pl.when(pl.program_id(0) == 0)
    def _():
        sums_ref[...] = jnp.zeros_like(sums_ref)

    sums_ref[...] += jnp.sum(total * x * factor, axis=0, keepdims=True)
    out_ref[...] = (mid_ref[...] + norm_back(total, x, factor, gain_ref[...])).astype(jnp.bfloat16)


def input_grad(place, pieces, weights, x, mid, gain):
    count, width = x.shape
    tile = 256
    row = lambda w: pl.BlockSpec((tile, w), lambda i, *_: (i, 0))
    whole = pl.BlockSpec(weights[0].shape, lambda i, *_: (0, 0), pipeline_mode=pl.Buffered(1))
    line = pl.BlockSpec((1, width), lambda i, *_: (0, 0))
    return pl.pallas_call(
        input_grad_kernel,
        out_shape=(
            jax.ShapeDtypeStruct((count, width), jnp.bfloat16),
            jax.ShapeDtypeStruct((1, width), jnp.float32),
        ),
        grid_spec=pltpu.PrefetchScalarGridSpec(
            num_scalar_prefetch=1,
            grid=(count // tile,),
            in_specs=[row(p.shape[1]) for p in pieces] + [whole] * 3 + [row(width), row(width), line],
            out_specs=[row(width), line],
        ),
        compiler_params=pltpu.CompilerParams(
            dimension_semantics=("arbitrary",), vmem_limit_bytes=48 << 20
        ),
        cost_estimate=pl.CostEstimate(
            flops=6 * count * width * width, transcendentals=count, bytes_accessed=22 * count * width
        ),
        name="input_grad",
    )(place, *pieces, *weights, x, mid, gain.reshape(1, width))


def swap(value, axis, size, bit=1):
    return lax.ppermute(value, axis, [(i, i ^ bit) for i in range(size)])


def pick(value, index, axis=0):
    return lax.dynamic_index_in_dim(value, index, axis, keepdims=False)


def in_order(bit, mine, theirs, axis=0):
    low = jnp.where(bit == 0, mine, theirs)
    high = jnp.where(bit == 0, theirs, mine)
    return jnp.stack([low, high], axis=axis)


class Place:
    def __init__(self, sizes):
        self.reps, self.groups, self.cores = sizes
        self.rep = lax.axis_index("rep")
        self.group = lax.axis_index("fsdp")
        self.core = lax.axis_index("ctx")
        self.paired = self.groups == 2 and self.cores == 2 and self.reps == 8


def put_rows(full, piece, at):
    return lax.dynamic_update_slice(full, piece, (at, jnp.zeros((), at.dtype)))


def gather_first(place, shards):
    if not place.paired:
        return [gather_rows(w) for w in shards], shards[-1]
    rows, cols = shards[0].shape
    half = rows // 2
    near = place.rep & 1
    group, core = place.group, place.core
    at = lambda g, c: (2 * g + c) * rows
    straight, around, fulls = [], [], []
    token = None
    for i, shard in enumerate(shards):
        sent = pick(shard.reshape(2, half, cols), near)
        if i > 0:
            sent, straight[i - 1] = lax.optimization_barrier((sent, straight[i - 1]))
        straight.append(swap(sent, "fsdp", 2))
    last = straight[-1]
    for i, shard in enumerate(shards):
        got = straight[i]
        more = swap(got, "rep", place.reps, 1)
        full = jnp.zeros((4 * rows, cols), shard.dtype)
        full = put_rows(full, shard, at(group, core))
        full = put_rows(full, swap(shard, "ctx", 2), at(group, 1 - core))
        full = put_rows(full, got, at(1 - group, core) + near * half)
        full = put_rows(full, swap(got, "ctx", 2), at(1 - group, 1 - core) + near * half)
        full = put_rows(full, more, at(1 - group, core) + (1 - near) * half)
        full = put_rows(full, swap(more, "ctx", 2), at(1 - group, 1 - core) + (1 - near) * half)
        fulls.append(full)
    return fulls, last


def gather_rows(shard):
    return lax.all_gather(shard, ("fsdp", "ctx"), axis=0, tiled=True)


def chip_sum(place, partial):
    total_rows, cols = partial.shape
    rows = total_rows // (place.groups * 2)
    blocks = partial.reshape(place.groups, 2, rows, cols)
    got = swap(pick(blocks, 1 - place.core, 1), "ctx", 2)
    return (pick(blocks, place.core, 1).astype(jnp.float32) + got.astype(jnp.float32)).astype(jnp.bfloat16)


def own_rows(place, value):
    if not place.paired:
        return lax.psum_scatter(value, "fsdp", scatter_dimension=0, tiled=True)[0]
    got = swap(pick(value, 1 - place.group), "fsdp", 2)
    return (pick(value, place.group).astype(jnp.float32) + got.astype(jnp.float32)).astype(jnp.bfloat16)


def spread_sum(place, value, order):
    groups, rows, cols = value.shape
    if not place.paired:
        mine = lax.psum_scatter(value, "fsdp", scatter_dimension=0, tiled=True)[0]
        return lax.psum(mine, "rep")
    bits = {"x": place.group, "y": place.rep & 1, "z": (place.rep >> 1) & 1}
    send = {
        "x": lambda v: swap(v, "fsdp", 2),
        "y": lambda v: swap(v, "rep", place.reps, 1),
        "z": lambda v: swap(v, "rep", place.reps, 2),
    }
    held = value.reshape(2, 2, 2, rows // 4, cols)
    axes = ["x", "y", "z"]
    for name in order:
        at = axes.index(name)
        got = send[name](pick(held, 1 - bits[name], at))
        held = (pick(held, bits[name], at).astype(jnp.float32) + got.astype(jnp.float32)).astype(jnp.bfloat16)
        axes.pop(at)
    held = (held.astype(jnp.float32) + swap(held, "rep", place.reps, 4).astype(jnp.float32)).astype(jnp.bfloat16)
    gathered = [name for name in reversed(order) if name != "x"]
    present = []
    for name in gathered:
        at = sum(1 for other in present if other < name)
        held = in_order(bits[name], held, send[name](held), axis=at)
        present.append(name)
    return held.reshape(rows, cols)


def everywhere_sum(place, value):
    if not place.paired:
        return lax.psum(value, ("rep", "fsdp", "ctx"))
    value = value + swap(value, "ctx", 2)
    value = value + swap(value, "fsdp", 2)
    for bit in (1, 2, 4):
        value = value + swap(value, "rep", place.reps, bit)
    return value


def shards(
    sizes,
    tokens,
    prefixes,
    query_weight,
    key_weight,
    value_weight,
    output_weight,
    up_weight,
    up_bias,
    down_weight,
    down_bias,
    attn_gain,
    mlp_gain,
    query_scale,
    cotangent,
):
    place = Place(sizes)
    core = place.core
    seq_count, local_rows, width = tokens.shape
    count = seq_count * local_rows
    part = width // 2
    heads_part = part // HD
    core_arg = core.astype(jnp.int32).reshape(1)

    (key_full, value_full, query_full), last = gather_first(place, [key_weight, value_weight, query_weight])
    output_shard, up_shard, down_shard, _ = lax.optimization_barrier((output_weight, up_weight, down_weight, last))
    output_full, up_full, down_full = [gather_rows(w) for w in (output_shard, up_shard, down_shard)]

    def columns(matrix, which):
        return lax.dynamic_slice_in_dim(matrix, which * part, part, axis=1)

    rows_in = tokens.reshape(count, width).astype(jnp.float32)
    factor_one = norm_factor(rows_in)
    normed = (rows_in * factor_one * attn_gain).astype(jnp.bfloat16)
    normed_all = jnp.concatenate([normed, swap(normed, "ctx", 2)], axis=0)
    scale_soft = jax.nn.softplus(query_scale) * (softplus_gain * HD ** (-0.5))
    scale_row = jnp.tile(scale_soft, heads_part)

    def split(value):
        return value.reshape(seq_count, local_rows, part)

    own, oth = [], []
    for matrix, scale in ((key_full, None), (value_full, None), (query_full, scale_row)):
        pair = [dot_nn(normed, columns(matrix, which)) for which in (core, 1 - core)]
        if scale is not None:
            pair = [v * scale for v in pair]
        pair = [split(v.astype(jnp.bfloat16)) for v in pair]
        own.append(pair[0])
        oth.append(swap(pair[1], "ctx", 2))
    own, oth = own[2:] + own[:2], oth[2:] + oth[:2]
    out_own, out_snd, lse = attention_forward(prefixes, core_arg, own, oth)
    out_rcv = swap(out_snd, "ctx", 2)

    attended = [out_own.reshape(count, part), out_rcv.reshape(count, part)]
    output_w = [
        lax.dynamic_slice_in_dim(output_full, which * part, part, axis=0) for which in (core, 1 - core)
    ]
    middle = rows_in + dot_nn(attended[0], output_w[0]) + dot_nn(attended[1], output_w[1])
    factor_two = norm_factor(middle)
    normed_two = (middle * factor_two * mlp_gain).astype(jnp.bfloat16)
    before = dot_nn(normed_two, up_full) + up_bias
    gate_sig = jax.nn.sigmoid(before)
    hidden = (before * gate_sig).astype(jnp.bfloat16)
    mixed_rows = middle + dot_nn(hidden, down_full) + down_bias
    mixed_out = mixed_rows.astype(jnp.bfloat16).reshape(seq_count, local_rows, width)

    upstream = cotangent.reshape(count, width)
    upstream_wide = upstream.astype(jnp.float32)

    def weight_grad(left, right):
        return lax.dot_general(
            left, right, (((0,), (0,)), ((), ())), preferred_element_type=jnp.float32
        ).astype(jnp.bfloat16)

    down_mine = own_rows(place, chip_sum(place, weight_grad(hidden, upstream)))
    downbias_part = jnp.sum(upstream_wide, axis=0)
    hidden_grad = dot_nt(upstream, down_full)
    before_grad = (hidden_grad * gate_sig * (1.0 + before * (1.0 - gate_sig))).astype(jnp.bfloat16)
    up_mine = own_rows(place, chip_sum(place, weight_grad(normed_two, before_grad)))
    upbias_part = jnp.sum(before_grad.astype(jnp.float32), axis=0)
    normed_grad = dot_nt(before_grad, up_full)
    mlpgain_part = jnp.sum(normed_grad * middle * factor_two, axis=0)
    middle_grad = upstream_wide + norm_back(normed_grad, middle, factor_two, mlp_gain)
    middle_low = middle_grad.astype(jnp.bfloat16)
    grad_own = dot_nt(middle_low, output_w[0]).astype(jnp.bfloat16)
    grad_snd = dot_nt(middle_low, output_w[1]).astype(jnp.bfloat16)
    grad_oth = swap(grad_snd, "ctx", 2)
    output_part = [weight_grad(a, middle_low) for a in attended]
    output_natural = in_order(core, output_part[0], output_part[1]).reshape(width, width)
    output_mine = own_rows(place, chip_sum(place, output_natural))
    early = everywhere_sum(place, jnp.stack([upbias_part, downbias_part, mlpgain_part]))

    back = functools.partial(
        attention_backward,
        prefixes,
        core_arg,
        own + [split(grad_own), out_own],
        oth + [split(grad_oth), out_snd],
        lse,
        scale_row.reshape(1, part),
    )
    heads_first = (heads_part * 5) // 8
    tiles_first = heads_first * HD // LANES
    *first, sums_first = back((0, heads_first), (0, tiles_first), ())
    grads_first, carry = first[:3], first[3:]

    def projection_grads(grads):
        return [weight_grad(normed_all, g.reshape(2 * count, g.shape[-1])) for g in grads]

    def received(grads):
        return [swap(g[1], "ctx", 2) for g in grads]

    partial_first = projection_grads(grads_first)
    other_first = received(grads_first)
    early_three = jnp.stack([down_mine, up_mine, output_mine])
    carry, partial_first, early_three, other_first = lax.optimization_barrier(
        (carry, partial_first, early_three, other_first)
    )
    early_total = lax.psum(early_three, "rep").astype(jnp.float32)
    down_total, up_total, output_total = early_total[0], early_total[1], early_total[2]

    *grads_last, sums_last = back((heads_first, heads_part), (tiles_first, part // LANES), carry)
    partial_last = projection_grads(grads_last)
    other_last = received(grads_last)

    totals = []
    for first_part, last_part, order in zip(partial_first, partial_last, ("xyz", "yzx", "zxy")):
        sides = []
        for value in (first_part, last_part):
            cols = value.shape[1]
            rows = width // place.groups
            mine = spread_sum(place, value.reshape(place.groups, rows, cols), order).reshape(2, rows // 2, cols)
            other = swap(pick(mine, 1 - core), "ctx", 2)
            sides.append((pick(mine, core), other))
        kept = jnp.concatenate([s[0] for s in sides], axis=1).astype(jnp.float32)
        came = jnp.concatenate([s[1] for s in sides], axis=1).astype(jnp.float32)
        totals.append(
            jnp.concatenate([jnp.where(core == 0, kept, came), jnp.where(core == 0, came, kept)], axis=1)
        )
    query_total, key_total, value_total = totals

    pieces = []
    for a, a_rcv, b, b_rcv in zip(grads_first, other_first, grads_last, other_last):
        for one in (a[0], b[0], a_rcv, b_rcv):
            pieces.append(one.reshape(count, one.shape[-1]))
    tokens_grad, attngain_part = input_grad(
        core_arg, pieces, [query_full, key_full, value_full], tokens.reshape(count, width), middle_grad, attn_gain
    )
    tokens_grad = tokens_grad.reshape(seq_count, local_rows, width)
    scale_part = jnp.sum((sums_first + sums_last).reshape(heads_part, HD), axis=0) / scale_soft
    scale_part = scale_part * jax.nn.sigmoid(query_scale) * (softplus_gain * HD ** (-0.5))
    late = everywhere_sum(place, jnp.concatenate([attngain_part.reshape(width), scale_part]))

    return (
        mixed_out,
        tokens_grad,
        query_total,
        key_total,
        value_total,
        output_total,
        up_total,
        early[0],
        down_total,
        early[1],
        late[:width],
        early[2],
        late[width:],
    )


def solution(mesh):
    sizes = (mesh.shape["rep"], mesh.shape["fsdp"], mesh.shape["ctx"])
    rows = P(("rep", "fsdp"), "ctx", None)
    weight = P(("fsdp", "ctx"), None)
    return jax.shard_map(
        functools.partial(shards, sizes),
        mesh=mesh,
        in_specs=(
            rows, P(("rep", "fsdp")), weight, weight, weight, weight, weight,
            P(), weight, P(), P(), P(), P(), rows,
        ),
        out_specs=(
            rows, rows, weight, weight, weight, weight, weight,
            P(), weight, P(), P(), P(), P(),
        ),
        check_vma=False,
    )
```

```python
import functools

import jax
import jax.numpy as jnp
from jax import lax
from jax.experimental import pallas as pl
from jax.experimental.pallas import tpu as pltpu
from jax.sharding import PartitionSpec as P


HD = 80
LANES = 128
WIN = 256
QB = 256

epsilon = 1e-06
softplus_gain = 1.442695041
masked_value = -1e30


def norm_factor(values):
    return lax.rsqrt(jnp.mean(values * values, axis=-1, keepdims=True) + epsilon)


def norm_back(upstream, values, factor, gain_vec):
    scaled = upstream * gain_vec
    row_inner = jnp.mean(scaled * values, axis=-1, keepdims=True)
    return factor * scaled - values * factor**3 * row_inner


def dot_nt(a, b):
    return lax.dot_general(a, b, (((1,), (1,)), ((), ())), preferred_element_type=jnp.float32)


def dot_nn(a, b):
    return lax.dot_general(a, b, (((1,), (0,)), ((), ())), preferred_element_type=jnp.float32)


def head_window(head, cols):
    start = jnp.minimum((head * HD) // LANES, cols // LANES - WIN // LANES)
    off = head * HD - start * LANES
    lane = lax.broadcasted_iota(jnp.int32, (1, WIN), 1)
    mask = (lane >= off) & (lane < off + HD)
    return pl.ds(pl.multiple_of(start * LANES, LANES), WIN), mask


def key_extent(block, half):
    return max(half, (block + 1) * QB)


def score_blocks(kw, qm, block, prefix, half):
    extent = key_extent(block, half)
    scores = dot_nt(kw[:extent], qm[block * QB : (block + 1) * QB])
    row = lax.broadcasted_iota(jnp.int32, (QB, QB), 0)
    col = lax.broadcasted_iota(jnp.int32, (QB, QB), 1)
    pieces = []
    for kb in range(extent // QB):
        piece = scores[kb * QB : (kb + 1) * QB]
        in_prefix = (row + kb * QB) < prefix
        if kb == block:
            allowed = row <= col
            if (kb * QB) < half:
                allowed = allowed | in_prefix
            piece = jnp.where(allowed, piece, masked_value)
        elif kb > block:
            piece = jnp.where(in_prefix, piece, masked_value)
        pieces.append(piece)
    return pieces


def forward_kernel(
    prefix_ref, place_ref,
    q_own, k_own, v_own, q_oth, k_oth, v_oth,
    o_own, o_oth, lse_ref,
    qs, ks, vs, os,
):
    seq, head = pl.program_id(0), pl.program_id(1)
    heads = pl.num_programs(1)
    half, cols = q_own.shape[1:]
    mine = pl.ds(pl.multiple_of(place_ref[0] * half, half), half)
    others = pl.ds(pl.multiple_of((1 - place_ref[0]) * half, half), half)

    @pl.when(head == 0)
    def _():
        for dst, a, b in ((qs, q_own, q_oth), (ks, k_own, k_oth), (vs, v_own, v_oth)):
            dst[mine, :] = a[0]
            dst[others, :] = b[0]

    prefix = prefix_ref[seq]
    win, mask = head_window(head, cols)
    kw = ks[:, win]
    zero = jnp.zeros((), qs.dtype)
    qm = jnp.where(mask, qs[:, win], zero)
    vt = vs[:, win].T
    for block in range(2 * half // QB):
        rows = slice(block * QB, (block + 1) * QB)
        pieces = score_blocks(kw, qm, block, prefix, half)
        top = functools.reduce(jnp.maximum, [jnp.max(p, axis=0, keepdims=True) for p in pieces])
        weights = [jnp.exp(p - top) for p in pieces]
        total = sum(jnp.sum(p, axis=0, keepdims=True) for p in weights)
        packed = jnp.concatenate([p.astype(jnp.bfloat16) for p in weights], axis=0)
        out_t = dot_nn(vt[:, : packed.shape[0]], packed) * (1.0 / total)
        out = out_t.T
        os[rows, win] = jnp.where(mask, out.astype(jnp.bfloat16), os[rows, win])
        lse_ref[0, pl.ds(head, 1), rows] = top + jnp.log(total)

    @pl.when(head == heads - 1)
    def _():
        o_own[0] = os[mine, :]
        o_oth[0] = os[others, :]


def backward_kernel(
    first_head, tiles, carried, prefix_ref, place_ref, *refs
):
    refs = list(refs)
    take = lambda n: [refs.pop(0) for _ in range(n)]
    q_own, k_own, v_own, g_own, o_own, q_oth, k_oth, v_oth, g_oth, o_oth = take(10)
    lse_ref, ind_ref, scale_ref = take(3)
    carry_in = take(1)[0] if carried else None
    grads, sent = take(2)
    carry_out = None if carried else take(1)[0]
    sums_ref = take(1)[0]
    qs, ks, vs, gs, dqs, dks, dvs, pbuf, sbuf, delta = refs
    seq, head = pl.program_id(0), pl.program_id(1) + first_head
    half, cols = q_own.shape[1:]
    start, stop = tiles[0] * LANES, tiles[1] * LANES
    mine = pl.ds(pl.multiple_of(place_ref[0] * half, half), half)
    others = pl.ds(pl.multiple_of((1 - place_ref[0]) * half, half), half)

    @pl.when(pl.program_id(1) == 0)
    def _():
        for dst, a, b in ((qs, q_own, q_oth), (ks, k_own, k_oth), (vs, v_own, v_oth), (gs, g_own, g_oth)):
            dst[mine, :] = a[0]
            dst[others, :] = b[0]
        for where_, g, o in ((mine, g_own, o_own), (others, g_oth, o_oth)):
            product = g[0].astype(jnp.float32) * o[0].astype(jnp.float32)
            high = product.astype(jnp.bfloat16)
            low = (product - high.astype(jnp.float32)).astype(jnp.bfloat16)
            delta[:, where_] = dot_nt(ind_ref[...], high) + dot_nt(ind_ref[...], low)
        if carried:
            for i, dst in enumerate((dqs, dks, dvs)):
                lanes = slice(i * LANES, (i + 1) * LANES)
                dst[mine, start : start + LANES] = carry_in[0, 0, :, lanes]
                dst[others, start : start + LANES] = carry_in[1, 0, :, lanes]

    @pl.when((seq == 0) & (pl.program_id(1) == 0))
    def _():
        sums_ref[...] = jnp.zeros_like(sums_ref)

    prefix = prefix_ref[seq]
    win, mask = head_window(head, cols)
    zero = jnp.zeros((), qs.dtype)
    kw = ks[:, win]
    vw = vs[:, win]
    qm = jnp.where(mask, qs[:, win], zero)
    gm = jnp.where(mask, gs[:, win], zero)
    kt = kw.T
    scale = scale_ref[:, win]
    blocks = 2 * half // QB
    for block in range(blocks):
        rows = slice(block * QB, (block + 1) * QB)
        extent = key_extent(block, half)
        pieces = score_blocks(kw, qm, block, prefix, half)
        pgrad = dot_nt(vw[:extent], gm[rows])
        lse = lse_ref[0, pl.ds(head, 1), rows]
        inner = delta[pl.ds(head, 1), rows]
        for kb, piece in enumerate(pieces):
            prob = jnp.exp(piece - lse)
            keys = slice(kb * QB, (kb + 1) * QB)
            pbuf[keys, rows] = prob.astype(jnp.bfloat16)
            sbuf[keys, rows] = (prob * (pgrad[keys] - inner)).astype(jnp.bfloat16)
        dq = dot_nn(kt[:, :extent], sbuf[:extent, rows]).T.astype(jnp.bfloat16).astype(jnp.float32)
        sums_ref[:, win] += jnp.sum(dq * qm[rows].astype(jnp.float32), axis=0, keepdims=True)
        dqs[rows, win] = jnp.where(mask, (dq * scale).astype(jnp.bfloat16), dqs[rows, win])
    for kb in range(blocks):
        keys = slice(kb * QB, (kb + 1) * QB)
        first = 0 if kb * QB < half else kb * QB
        dv = dot_nn(pbuf[keys, first:], gm[first:])
        dvs[keys, win] = jnp.where(mask, dv.astype(jnp.bfloat16), dvs[keys, win])
        dk = dot_nn(sbuf[keys, first:], qm[first:])
        dks[keys, win] = jnp.where(mask, dk.astype(jnp.bfloat16), dks[keys, win])

    @pl.when(pl.program_id(1) == pl.num_programs(1) - 1)
    def _():
        wide = stop - start
        for i, src in enumerate((dqs, dks, dvs)):
            cut = slice(i * wide, (i + 1) * wide)
            grads[0, 0, :, cut] = src[mine, start:stop]
            away = src[others, start:stop]
            grads[1, 0, :, cut] = away
            sent[0, :, cut] = away
            if not carried:
                lanes = slice(i * LANES, (i + 1) * LANES)
                carry_out[0, 0, :, lanes] = src[mine, stop : stop + LANES]
                carry_out[1, 0, :, lanes] = src[others, stop : stop + LANES]


def seq_spec(half, cols):
    return pl.BlockSpec((1, half, cols), lambda s, h, *_: (s, 0, 0))


def attention_forward(prefixes, place, own, oth):
    seqs, half, cols = own[0].shape
    heads = cols // HD
    spec = seq_spec(half, cols)
    piece = jax.ShapeDtypeStruct((seqs, half, cols), jnp.bfloat16)
    length = 2 * half
    cells = seqs * heads * length * length
    return pl.pallas_call(
        forward_kernel,
        out_shape=(piece, piece, jax.ShapeDtypeStruct((seqs, heads, length), jnp.float32)),
        grid_spec=pltpu.PrefetchScalarGridSpec(
            num_scalar_prefetch=2,
            grid=(seqs, heads),
            in_specs=[spec] * 6,
            out_specs=[spec, spec, pl.BlockSpec((1, heads, length), lambda s, h, *_: (s, 0, 0))],
            scratch_shapes=[pltpu.VMEM((length, cols), jnp.bfloat16)] * 4,
        ),
        compiler_params=pltpu.CompilerParams(
            dimension_semantics=("arbitrary", "arbitrary"), vmem_limit_bytes=56 << 20
        ),
        cost_estimate=pl.CostEstimate(
            flops=2 * cells * WIN * 2, transcendentals=cells, bytes_accessed=8 * seqs * half * cols * 2
        ),
        name="attention_forward",
    )(prefixes, place, *own, *oth)


def attention_backward(prefixes, place, own, oth, lse, scale, heads_of, tiles, carry):
    seqs, half, cols = own[0].shape
    heads = cols // HD
    spec = seq_spec(half, cols)
    length = 2 * half
    cells = seqs * (heads_of[1] - heads_of[0]) * length * length
    indicator = (
        jnp.arange(heads, dtype=jnp.int32)[:, None] == (jnp.arange(cols, dtype=jnp.int32) // HD)[None, :]
    ).astype(jnp.bfloat16)

    def grad(width):
        shape = jax.ShapeDtypeStruct((2, seqs, half, width), jnp.bfloat16)
        return shape, pl.BlockSpec((2, 1, half, width), lambda s, h, *_: (0, s, 0, 0))

    width = (tiles[1] - tiles[0]) * LANES
    outs = [grad(3 * width)]
    outs.append((jax.ShapeDtypeStruct((seqs, half, 3 * width), jnp.bfloat16), seq_spec(half, 3 * width)))
    if not carry:
        outs.append(grad(3 * LANES))
    outs.append((jax.ShapeDtypeStruct((1, cols), jnp.float32), pl.BlockSpec((1, cols), lambda s, h, *_: (0, 0))))
    return pl.pallas_call(
        functools.partial(backward_kernel, heads_of[0], tiles, bool(carry)),
        out_shape=[o[0] for o in outs],
        grid_spec=pltpu.PrefetchScalarGridSpec(
            num_scalar_prefetch=2,
            grid=(seqs, heads_of[1] - heads_of[0]),
            in_specs=[spec] * 10
            + [
                pl.BlockSpec((1, heads, length), lambda s, h, *_: (s, 0, 0)),
                pl.BlockSpec((heads, cols), lambda s, h, *_: (0, 0)),
                pl.BlockSpec((1, cols), lambda s, h, *_: (0, 0)),
            ]
            + [grad(3 * LANES)[1]] * len(carry),
            out_specs=[o[1] for o in outs],
            scratch_shapes=[pltpu.VMEM((length, cols), jnp.bfloat16)] * 7
            + [pltpu.VMEM((length, length), jnp.bfloat16)] * 2
            + [pltpu.VMEM((heads, length), jnp.float32)],
        ),
        compiler_params=pltpu.CompilerParams(
            dimension_semantics=("arbitrary", "arbitrary"), vmem_limit_bytes=60 << 20
        ),
        cost_estimate=pl.CostEstimate(
            flops=2 * cells * WIN * 5, transcendentals=cells, bytes_accessed=16 * seqs * half * cols * 2
        ),
        name="attention_backward",
    )(prefixes, place, *own, *oth, lse, indicator, scale, *carry)


def input_grad_kernel(first, place_ref, *refs):
    if not first:
        refs = refs[1:]
    own_a, own_b, oth_a, oth_b, wq, wk, wv, x_ref, mid_ref, gain_ref, out_ref, sums_ref = refs
    part = wq.shape[1] // 2
    total = None
    for i, weight in enumerate((wq, wk, wv)):
        for side, pair in enumerate(((own_a, own_b), (oth_a, oth_b))):
            base = jnp.where(place_ref[0] == side, 0, part)
            at = 0
            for ref in pair:
                width = ref.shape[-1] // 3
                cut = slice(i * width, (i + 1) * width)
                piece = ref[0, :, cut] if len(ref.shape) == 3 else ref[:, cut]
                window = weight[:, pl.ds(pl.multiple_of(base + at, LANES), width)]
                term = dot_nt(piece, window)
                total = term if total is None else total + term
                at += width
    x = x_ref[...].astype(jnp.float32)
    factor = norm_factor(x)

    @pl.when(pl.program_id(0) == 0)
    def _():
        sums_ref[...] = jnp.zeros_like(sums_ref)

    sums_ref[...] += jnp.sum(total * x * factor, axis=0, keepdims=True)
    out_ref[...] = (mid_ref[...] + norm_back(total, x, factor, gain_ref[...])).astype(jnp.bfloat16)


def input_grad(place, own, oth, weights, x, mid, gain, share, before):
    count, width = x.shape
    tile = 256
    steps = count // tile // 2
    skip = share * steps
    row = lambda w: pl.BlockSpec((tile, w), lambda i, *_: (i + skip, 0))
    front = lambda w: pl.BlockSpec((1, tile, w), lambda i, *_: (0, i + skip, 0))
    whole = pl.BlockSpec(weights[0].shape, lambda i, *_: (0, 0), pipeline_mode=pl.Buffered(1))
    line = pl.BlockSpec((1, width), lambda i, *_: (0, 0))
    return pl.pallas_call(
        functools.partial(input_grad_kernel, before is None),
        out_shape=(
            jax.ShapeDtypeStruct((count, width), jnp.bfloat16),
            jax.ShapeDtypeStruct((1, width), jnp.float32),
        ),
        grid_spec=pltpu.PrefetchScalarGridSpec(
            num_scalar_prefetch=1,
            grid=(steps,),
            in_specs=([] if before is None else [pl.BlockSpec(memory_space=pl.ANY)])
            + [front(p.shape[2]) for p in own]
            + [row(p.shape[1]) for p in oth]
            + [whole] * 3
            + [row(width), row(width), line],
            out_specs=[row(width), line],
        ),
        input_output_aliases={} if before is None else {1: 0},
        compiler_params=pltpu.CompilerParams(
            dimension_semantics=("arbitrary",), vmem_limit_bytes=48 << 20
        ),
        cost_estimate=pl.CostEstimate(
            flops=3 * count * width * width, transcendentals=count, bytes_accessed=11 * count * width
        ),
        name="input_grad",
    )(place, *([] if before is None else [before]), *own, *oth, *weights, x, mid, gain.reshape(1, width))


def swap(value, axis, size, bit=1):
    return lax.ppermute(value, axis, [(i, i ^ bit) for i in range(size)])


def pick(value, index, axis=0):
    return lax.dynamic_index_in_dim(value, index, axis, keepdims=False)


def in_order(bit, mine, theirs, axis=0):
    low = jnp.where(bit == 0, mine, theirs)
    high = jnp.where(bit == 0, theirs, mine)
    return jnp.stack([low, high], axis=axis)


class Place:
    def __init__(self, sizes):
        self.reps, self.groups, self.cores = sizes
        self.rep = lax.axis_index("rep")
        self.group = lax.axis_index("fsdp")
        self.core = lax.axis_index("ctx")
        self.paired = self.groups == 2 and self.cores == 2 and self.reps == 8


def put_rows(full, piece, at):
    return lax.dynamic_update_slice(full, piece, (at, jnp.zeros((), at.dtype)))


def gather_first(place, shards):
    if not place.paired:
        return [gather_rows(w) for w in shards], shards[-1]
    rows, cols = shards[0].shape
    half = rows // 2
    near = place.rep & 1
    group, core = place.group, place.core
    at = lambda g, c: (2 * g + c) * rows
    straight, fulls = [], []
    for i, shard in enumerate(shards):
        sent = pick(shard.reshape(2, half, cols), near)
        if i > 0:
            sent, straight[i - 1] = lax.optimization_barrier((sent, straight[i - 1]))
        straight.append(swap(sent, "fsdp", 2))
    last = straight[-1]
    for i, shard in enumerate(shards):
        got = straight[i]
        more = swap(got, "rep", place.reps, 1)
        full = jnp.zeros((4 * rows, cols), shard.dtype)
        full = put_rows(full, shard, at(group, core))
        full = put_rows(full, swap(shard, "ctx", 2), at(group, 1 - core))
        full = put_rows(full, got, at(1 - group, core) + near * half)
        full = put_rows(full, swap(got, "ctx", 2), at(1 - group, 1 - core) + near * half)
        full = put_rows(full, more, at(1 - group, core) + (1 - near) * half)
        full = put_rows(full, swap(more, "ctx", 2), at(1 - group, 1 - core) + (1 - near) * half)
        fulls.append(full)
    return fulls, last


def gather_rows(shard):
    return lax.all_gather(shard, ("fsdp", "ctx"), axis=0, tiled=True)


def chip_sum(place, partial):
    total_rows, cols = partial.shape
    rows = total_rows // (place.groups * 2)
    blocks = partial.reshape(place.groups, 2, rows, cols)
    got = swap(pick(blocks, 1 - place.core, 1), "ctx", 2)
    return (pick(blocks, place.core, 1).astype(jnp.float32) + got.astype(jnp.float32)).astype(jnp.bfloat16)


def own_rows(place, value):
    if not place.paired:
        return lax.psum_scatter(value, "fsdp", scatter_dimension=0, tiled=True)[0]
    got = swap(pick(value, 1 - place.group), "fsdp", 2)
    return (pick(value, place.group).astype(jnp.float32) + got.astype(jnp.float32)).astype(jnp.bfloat16)


def mixed_swap(place, value, kinds):
    pairs = []
    for rep in range(place.reps):
        for group in range(place.groups):
            for core, kind in enumerate(kinds):
                to = (rep ^ kind, group) if kind else (rep, group ^ 1)
                index = lambda r, g: (r * place.groups + g) * place.cores + core
                pairs.append((index(rep, group), index(*to)))
    return lax.ppermute(value, ("rep", "fsdp", "ctx"), pairs)


def spread_sum(place, value):
    total_rows, cols = value.shape
    if not place.paired:
        mine = lax.psum_scatter(value, "fsdp", scatter_dimension=0, tiled=True)
        return lax.psum(mine, "rep")
    add = lambda a, b: (a.astype(jnp.float32) + b.astype(jnp.float32)).astype(jnp.bfloat16)
    rows = total_rows // 8
    even = place.core == 0
    group, low, high = place.group, place.rep & 1, (place.rep >> 1) & 1
    blocks = value.reshape(8, rows, cols)

    def half(side):
        starts = jnp.where(even, 4 * side, 2 * side), jnp.where(even, 4 * side + 2, 2 * side + 4)
        return jnp.stack([lax.dynamic_slice_in_dim(blocks, s, 2) for s in starts])

    first = jnp.where(even, group, high)
    second = jnp.where(even, low, group)
    third = jnp.where(even, high, low)
    held = add(half(first), mixed_swap(place, half(1 - first), (0, 2)))
    for bit, kinds in ((second, (1, 0)), (third, (2, 1))):
        held = add(pick(held, bit), mixed_swap(place, pick(held, 1 - bit), kinds))
    held = add(held, mixed_swap(place, held, (4, 4)))
    held = in_order(third, held, mixed_swap(place, held, (2, 1)))
    last = jnp.where(even, low, high)
    held = in_order(last, held, mixed_swap(place, held, (1, 2)))
    return held.reshape(4 * rows, cols)


def everywhere_sum(place, value):
    if not place.paired:
        return lax.psum(value, ("rep", "fsdp", "ctx"))
    value = value + swap(value, "ctx", 2)
    value = value + swap(value, "fsdp", 2)
    for bit in (1, 2, 4):
        value = value + swap(value, "rep", place.reps, bit)
    return value


def shards(sizes, *arrays):
    return layer(Place(sizes), *arrays)


def layer(
    place,
    tokens,
    prefixes,
    query_weight,
    key_weight,
    value_weight,
    output_weight,
    up_weight,
    up_bias,
    down_weight,
    down_bias,
    attn_gain,
    mlp_gain,
    query_scale,
    cotangent,
):
    core = place.core
    seq_count, local_rows, width = tokens.shape
    count = seq_count * local_rows
    part = width // 2
    heads_part = part // HD
    core_arg = core.astype(jnp.int32).reshape(1)

    (key_full, value_full, query_full), last = gather_first(place, [key_weight, value_weight, query_weight])
    output_shard, up_shard, down_shard, _ = lax.optimization_barrier((output_weight, up_weight, down_weight, last))
    output_full, up_full, down_full = [gather_rows(w) for w in (output_shard, up_shard, down_shard)]

    def columns(matrix, which):
        return lax.dynamic_slice_in_dim(matrix, which * part, part, axis=1)

    rows_in = tokens.reshape(count, width).astype(jnp.float32)
    factor_one = norm_factor(rows_in)
    normed = (rows_in * factor_one * attn_gain).astype(jnp.bfloat16)
    normed_all = jnp.concatenate([normed, swap(normed, "ctx", 2)], axis=0)
    scale_soft = jax.nn.softplus(query_scale) * (softplus_gain * HD ** (-0.5))
    scale_row = jnp.tile(scale_soft, heads_part)

    def split(value):
        return value.reshape(seq_count, local_rows, part)

    own, oth = [], []
    for matrix, scale in ((key_full, None), (value_full, None), (query_full, scale_row)):
        pair = [dot_nn(normed, columns(matrix, which)) for which in (core, 1 - core)]
        if scale is not None:
            pair = [v * scale for v in pair]
        pair = [split(v.astype(jnp.bfloat16)) for v in pair]
        own.append(pair[0])
        oth.append(swap(pair[1], "ctx", 2))
    own, oth = own[2:] + own[:2], oth[2:] + oth[:2]
    out_own, out_snd, lse = attention_forward(prefixes, core_arg, own, oth)
    out_rcv = swap(out_snd, "ctx", 2)

    attended = [out_own.reshape(count, part), out_rcv.reshape(count, part)]
    output_w = [
        lax.dynamic_slice_in_dim(output_full, which * part, part, axis=0) for which in (core, 1 - core)
    ]
    middle = rows_in + dot_nn(attended[0], output_w[0]) + dot_nn(attended[1], output_w[1])
    factor_two = norm_factor(middle)
    normed_two = (middle * factor_two * mlp_gain).astype(jnp.bfloat16)
    before = dot_nn(normed_two, up_full) + up_bias
    gate_sig = jax.nn.sigmoid(before)
    hidden = (before * gate_sig).astype(jnp.bfloat16)
    mixed_rows = middle + dot_nn(hidden, down_full) + down_bias
    mixed_out = mixed_rows.astype(jnp.bfloat16).reshape(seq_count, local_rows, width)

    upstream = cotangent.reshape(count, width)
    upstream_wide = upstream.astype(jnp.float32)

    def weight_grad(left, right):
        return lax.dot_general(
            left, right, (((0,), (0,)), ((), ())), preferred_element_type=jnp.float32
        ).astype(jnp.bfloat16)

    down_mine = own_rows(place, chip_sum(place, weight_grad(hidden, upstream)))
    downbias_part = jnp.sum(upstream_wide, axis=0)
    hidden_grad = dot_nt(upstream, down_full)
    before_grad = (hidden_grad * gate_sig * (1.0 + before * (1.0 - gate_sig))).astype(jnp.bfloat16)
    up_mine = own_rows(place, chip_sum(place, weight_grad(normed_two, before_grad)))
    upbias_part = jnp.sum(before_grad.astype(jnp.float32), axis=0)
    normed_grad = dot_nt(before_grad, up_full)
    mlpgain_part = jnp.sum(normed_grad * middle * factor_two, axis=0)
    middle_grad = upstream_wide + norm_back(normed_grad, middle, factor_two, mlp_gain)
    middle_low = middle_grad.astype(jnp.bfloat16)
    grad_own = dot_nt(middle_low, output_w[0]).astype(jnp.bfloat16)
    grad_snd = dot_nt(middle_low, output_w[1]).astype(jnp.bfloat16)
    grad_oth = swap(grad_snd, "ctx", 2)
    output_part = [weight_grad(a, middle_low) for a in attended]
    output_natural = in_order(core, output_part[0], output_part[1]).reshape(width, width)
    output_mine = own_rows(place, chip_sum(place, output_natural))
    early = everywhere_sum(place, jnp.stack([upbias_part, downbias_part, mlpgain_part]))

    back = functools.partial(
        attention_backward,
        prefixes,
        core_arg,
        own + [split(grad_own), out_own],
        oth + [split(grad_oth), out_snd],
        lse,
        scale_row.reshape(1, part),
    )
    heads_first = (heads_part * 5) // 8
    tiles_first = heads_first * HD // LANES
    grads_first, send_first, carry, sums_first = back((0, heads_first), (0, tiles_first), ())

    def projection_grads(grads):
        return weight_grad(normed_all, grads.reshape(2 * count, grads.shape[-1]))

    partial_first = projection_grads(grads_first)
    other_first = swap(send_first, "ctx", 2)
    early_three = jnp.stack([down_mine, up_mine, output_mine])
    carry, partial_first, early_three = lax.optimization_barrier((carry, partial_first, early_three))
    early_total = lax.psum(early_three, "rep").astype(jnp.float32)
    down_total, up_total, output_total = early_total[0], early_total[1], early_total[2]

    grads_last, send_last, sums_last = back((heads_first, heads_part), (tiles_first, part // LANES), (carry,))
    partial_last = projection_grads(grads_last)
    other_last = swap(send_last, "ctx", 2)

    sides = []
    for value in (partial_first, partial_last):
        mine = spread_sum(place, value).reshape(2, -1, value.shape[1])
        other = swap(pick(mine, 1 - core), "ctx", 2)
        sides.append((pick(mine, core), other))

    def columns_of(which):
        pieces = []
        for i in range(3):
            cut = [s[which][:, i * (s[which].shape[1] // 3) : (i + 1) * (s[which].shape[1] // 3)] for s in sides]
            pieces.append(jnp.concatenate(cut, axis=1).astype(jnp.float32))
        return pieces

    query_total, key_total, value_total = [
        jnp.concatenate([jnp.where(core == 0, kept, came), jnp.where(core == 0, came, kept)], axis=1)
        for kept, came in zip(columns_of(0), columns_of(1))
    ]

    tokens_grad, attngain_part = None, 0.0
    for share in range(2):
        tokens_grad, sums = input_grad(
            core_arg,
            [g.reshape(2, count, g.shape[-1]) for g in (grads_first, grads_last)],
            [g.reshape(count, g.shape[-1]) for g in (other_first, other_last)],
            [query_full, key_full, value_full],
            tokens.reshape(count, width),
            middle_grad,
            attn_gain,
            share,
            tokens_grad,
        )
        attngain_part = attngain_part + sums.reshape(width)
    tokens_grad = tokens_grad.reshape(seq_count, local_rows, width)
    scale_part = jnp.sum((sums_first + sums_last).reshape(heads_part, HD), axis=0) / scale_soft
    scale_part = scale_part * jax.nn.sigmoid(query_scale) * (softplus_gain * HD ** (-0.5))
    late = everywhere_sum(place, jnp.concatenate([attngain_part, scale_part]))

    return (
        mixed_out,
        tokens_grad,
        query_total,
        key_total,
        value_total,
        output_total,
        up_total,
        early[0],
        down_total,
        early[1],
        late[:width],
        early[2],
        late[width:],
    )


def solution(mesh):
    sizes = (mesh.shape["rep"], mesh.shape["fsdp"], mesh.shape["ctx"])
    rows = P(("rep", "fsdp"), "ctx", None)
    weight = P(("fsdp", "ctx"), None)
    return jax.shard_map(
        functools.partial(shards, sizes),
        mesh=mesh,
        in_specs=(
            rows, P(("rep", "fsdp")), weight, weight, weight, weight, weight,
            P(), weight, P(), P(), P(), P(), rows,
        ),
        out_specs=(
            rows, rows, weight, weight, weight, weight, weight,
            P(), weight, P(), P(), P(), P(),
        ),
        check_vma=False,
    )
```
